32 devices in a mesh: grp: 2 (over y), pb: 4 (over z), re: 2 (over x), ka: 2 (over core).
Axes of the slice: x: 2, y: 2, z: 4, core: 2. Of those that a mesh axis runs over, the one named last changes fastest.
Arguments:
- g_wann: bfloat16 [2, 1024, 128, 256], P(None, 'pb', ('grp', 're'), 'ka'), parts along dimension 2, may hold values from -0.0234375 to 0.0234375
- phonon_phase: bfloat16 [2, 2048, 1024], P(None, 'pb'), may hold values from -1 to 1, as said below
- electron_phase: bfloat16 [2, 8, 64], replicated, may hold values from -1 to 1, as said below
Outputs:
- coupling: float32 [16, 2, 2048, 256], P(('grp', 're'), None, 'pb', 'ka'), parts along dimension 0
The draws below stay inside these ranges and needn't reach their ends.
There are 2 independent parts, one for each index of `grp`. The reference program is written for one: setup_inputs(seed, part) draws one part's arguments, and reference() takes and returns one part's arrays. A program takes and returns all parts, laid end to end along the dimension named above; an argument that names none is the same for every part. Nothing has to cross between parts.
Inputs may be any that keep to these rules, and one draw needn't show every extreme that they name: `phonon_phase`: entries 0 and 1 along the first dimension are the cosine and sine of one angle. `electron_phase`: entries 0 and 1 along the first dimension are the cosine and sine of one angle.
All inputs are finite; a program needn't handle non-finite values.
Results may differ from the reference program's by a relative error of at most 0.0029.
Values may be sent and summed in bfloat16 or wider, within the bound.
A program may use at most 64 MiB of HBM per device.

```python
import math
import jax
import jax.numpy as jnp
from jax import lax

BP = 256
RP = 1024
RE = 64
Q = 2048
K = 8


def phase_table(key, rows, vectors):
    key_moment, key_vector = jax.random.split(key)
    moment = jax.random.uniform(key_moment, (rows, 3), jnp.float32)
    picked = jax.random.permutation(key_vector, 4096)[:vectors]
    first = (picked // 256 - 8).astype(jnp.float32)
    second = (picked // 16 % 16 - 8).astype(jnp.float32)
    third = (picked % 16 - 8).astype(jnp.float32)
    product = moment[:, 0:1] * first[None, :] + moment[:, 1:2] * second[None, :] + moment[:, 2:3] * third[None, :]
    angle = 2.0 * math.pi * product
    return jnp.stack([jnp.cos(angle), jnp.sin(angle)]).astype(jnp.bfloat16)


def draw_phonon_phase(key, part):
    return phase_table(jax.random.fold_in(key, 101), Q, RP)


def draw_electron_phase(key, part):
    return phase_table(jax.random.fold_in(key, 202), K, RE)


def levels(key, extent, shards, low, largest):
    loudness = 1.0
    for axis_at, blocks in shards:
        steps = jax.random.uniform(jax.random.fold_in(jax.random.fold_in(key, 6), axis_at), (blocks,), jnp.float32, low / len(shards), largest / len(shards))
        loudness = loudness * jnp.repeat(jnp.exp(steps), extent[axis_at] // blocks).reshape((-1,) + (1,) * (len(extent) - 1 - axis_at))
    return loudness


def centred(stream_key, dims, width, bound, cuts=(), kind=jnp.bfloat16):
    drawn = jax.random.normal(stream_key, dims, jnp.float32) * width
    if len(cuts) > 0:
        drawn = levels(stream_key, dims, cuts, -0.22, 0.18) * drawn
    return jnp.clip(drawn, min=-bound, max=bound).astype(kind)


def setup_inputs(seed: int = 0, part: int = 0) -> dict:
    streams_of = jax.random.split(jax.random.key(seed), 4)
    part_keys = jax.random.split(jax.random.fold_in(streams_of[3], part), 4)
    return {
        "g_wann": centred(part_keys[0], (2, RP, RE, BP), (RE * RP) ** -0.5, 0.0234375, ((1, 4), (2, 2), (3, 2))),
        "phonon_phase": draw_phonon_phase(jax.random.fold_in(streams_of[3], 71), part),
        "electron_phase": draw_electron_phase(jax.random.fold_in(streams_of[3], 71), part),
    }


def reference(g_wann, phonon_phase, electron_phase):
    elec_cos = electron_phase[0].astype(jnp.float32)
    elec_sin = electron_phase[1].astype(jnp.float32)
    wann_real = g_wann[0].astype(jnp.float32)
    wann_imag = g_wann[1].astype(jnp.float32)
    high = lax.Precision.HIGHEST
    bloch_real = jnp.einsum("ke,peb->kpb", elec_cos, wann_real, precision=high) - jnp.einsum("ke,peb->kpb", elec_sin, wann_imag, precision=high)
    bloch_imag = jnp.einsum("ke,peb->kpb", elec_cos, wann_imag, precision=high) + jnp.einsum("ke,peb->kpb", elec_sin, wann_real, precision=high)
    bloch_real = bloch_real.astype(jnp.bfloat16)
    bloch_imag = bloch_imag.astype(jnp.bfloat16)
    cos_table = phonon_phase[0]
    sin_table = phonon_phase[1]

    def one_moment(pair):
        part_real, part_imag = pair
        out_real = jnp.dot(cos_table, part_real, preferred_element_type=jnp.float32) - jnp.dot(sin_table, part_imag, preferred_element_type=jnp.float32)
        out_imag = jnp.dot(cos_table, part_imag, preferred_element_type=jnp.float32) + jnp.dot(sin_table, part_real, preferred_element_type=jnp.float32)
        return jnp.stack([out_real, out_imag])

    return lax.map(one_moment, (bloch_real, bloch_imag))
```

```python
import functools
import jax
import jax.numpy as jnp
from jax import lax
from jax.experimental import pallas as pl
from jax.experimental.pallas import tpu as pltpu
from jax.sharding import PartitionSpec as P

MESH = pl.DeviceIdType.MESH
GROUP = 8
PAIR = 2
UNROLL = 4
AHEAD = 1
SLACK = 0
EARLY = 3
OWN_AHEAD = 5
PIECES = 4
LAG = 2
BF16 = jnp.bfloat16
F32 = jnp.float32


def iota(shape, dim):
    return lax.broadcasted_iota(jnp.int32, shape, dim)


def kernel(
    n_re, n_pb, halves,
    g_hbm, ph_hbm, el_hbm, out,
    g, ph, el_ref, el_block, part, x_first, x_first_recv, x_recv, gath,
    g_sem, ph_sem, el_sem, x_send, x_got, z_send, z_got,
):
    x = lax.axis_index("re")
    z = lax.axis_index("pb")
    k_all, p_loc, width = part.shape
    b = width // 2
    k_own = k_all // n_re
    p_half = p_loc // halves
    e_all = el_ref.shape[2]
    e_loc = g.shape[1] // p_loc
    chunks = k_own * halves
    q_loc = ph.shape[1]

    def g_copy(h):
        rows = pl.ds(h * p_half * e_loc, p_half * e_loc)
        return pltpu.make_async_copy(g_hbm.at[:, rows, :], g.at[:, rows, :], g_sem.at[h])

    barrier = pltpu.get_barrier_semaphore()
    for d in range(1, n_re):
        pl.semaphore_signal(barrier, inc=1, device_id={"re": lax.rem(x + d, n_re)}, device_id_type=MESH)

    @pl.when(z > 0)
    def _():
        pl.semaphore_signal(barrier, inc=1, device_id={"pb": z - 1}, device_id_type=MESH)

    @pl.when(z < n_pb - 1)
    def _():
        pl.semaphore_signal(barrier, inc=1, device_id={"pb": z + 1}, device_id_type=MESH)

    el_copy = pltpu.make_async_copy(el_hbm, el_ref, el_sem)
    el_copy.start()
    for h in range(halves):
        g_copy(h).start()

    rows, cols = k_all * GROUP, GROUP * e_loc
    spread_k = (iota((rows, k_all), 0) // GROUP == iota((rows, k_all), 1)).astype(BF16)
    spread_e = (iota((e_all, cols), 0) == x * e_loc + iota((e_all, cols), 1) % e_loc).astype(BF16)
    same_p = iota((rows, cols), 0) % GROUP == iota((rows, cols), 1) // e_loc

    def spread(table):
        t = jnp.dot(spread_k, table, preferred_element_type=F32).astype(BF16)
        t = jnp.dot(t, spread_e, preferred_element_type=F32)
        return jnp.where(same_p, t, 0.0)

    el_copy.wait()
    cos_e = spread(el_ref[0])
    sin_e = spread(el_ref[1])
    el_block[0:rows, 0:cols] = cos_e.astype(BF16)
    el_block[0:rows, cols:] = (-sin_e).astype(BF16)
    el_block[rows:, 0:cols] = sin_e.astype(BF16)
    el_block[rows:, cols:] = cos_e.astype(BF16)

    def x_first_copy(h, d):
        there = pl.ds(pl.multiple_of(h * p_half, p_half), p_half)
        to = lax.rem(x + d, n_re)
        return pltpu.make_async_remote_copy(
            src_ref=x_first.at[to, there, :],
            dst_ref=x_first_recv.at[d - 1, there, :],
            send_sem=x_send.at[d - 1, h],
            recv_sem=x_got.at[d - 1, h],
            device_id={"re": to},
            device_id_type=MESH,
        )

    def x_copy(c, d):
        k, h = c // halves, c % halves
        there = pl.ds(pl.multiple_of(h * p_half, p_half), p_half)
        to = lax.rem(x + d, n_re)
        return pltpu.make_async_remote_copy(
            src_ref=part.at[to * k_own + k, there, :],
            dst_ref=x_recv.at[d - 1, k, there, :],
            send_sem=x_send.at[d - 1, c],
            recv_sem=x_got.at[d - 1, c],
            device_id={"re": to},
            device_id_type=MESH,
        )

    def z_copy(c, source, way):
        k, h = c // halves, c % halves
        there = pl.ds(pl.multiple_of(source * p_loc + h * p_half, p_half), p_half)
        block = gath.at[k, there, :]
        return pltpu.make_async_remote_copy(
            src_ref=block,
            dst_ref=block,
            send_sem=z_send.at[way, c, source],
            recv_sem=z_got.at[c, source],
            device_id={"pb": z + 1 if way else z - 1},
            device_id_type=MESH,
        )

    def own_step(t):
        k, h = t // halves, t % halves
        there = pl.ds(pl.multiple_of(h * p_half, p_half), p_half)
        mine = pl.ds(pl.multiple_of(z * p_loc + h * p_half, p_half), p_half)

        @pl.when(t < halves)
        def _():
            total = part[x * k_own, there, :]
            for d in range(1, n_re):
                x_first_copy(t, d).wait_recv()
                total = total + x_first_recv[d - 1, there, :].astype(F32)
            gath[0, mine, :] = total.astype(BF16)

        @pl.when(t >= halves)
        def _():
            total = part[x * k_own + k, there, :]
            for d in range(1, n_re):
                x_copy(t, d).wait_recv()
                total = total + x_recv[d - 1, k, there, :]
            gath[k, mine, :] = total.astype(BF16)

        @pl.when(z > 0)
        def _():
            z_copy(t, z, 0).start()

        @pl.when(z < n_pb - 1)
        def _():
            z_copy(t, z, 1).start()

    for h in range(halves):
        g_copy(h).wait()

        @pl.loop(h * (p_half // GROUP // PAIR), (h + 1) * (p_half // GROUP // PAIR), unroll=UNROLL)
        def _(j):
            sides = []
            for side in range(PAIR):
                at = pl.ds(pl.multiple_of((j * PAIR + side) * cols, cols), cols)
                sides.append(jnp.concatenate([g[0, at, :], g[1, at, :]], axis=0))
            both = jnp.concatenate(sides, axis=1)
            res = jnp.dot(el_block[...], both, preferred_element_type=F32)
            for side in range(PAIR):
                p_at = pl.ds(pl.multiple_of((j * PAIR + side) * GROUP, GROUP), GROUP)
                for c in range(2):
                    for k in range(k_all):
                        first = (c * k_all + k) * GROUP
                        part[k, p_at, c * b:(c + 1) * b] = res[first:first + GROUP, side * b:(side + 1) * b]

        if h == 0:
            n_meet = n_re - 1 + jnp.where(z > 0, 1, 0) + jnp.where(z < n_pb - 1, 1, 0)
            pl.semaphore_wait(barrier, n_meet)
        there = pl.ds(h * p_half, p_half)
        for r in range(n_re):
            x_first[r, there, :] = part[r * k_own, there, :].astype(BF16)
        for d in range(1, n_re):
            x_first_copy(h, d).start()
        if h >= halves - AHEAD:
            own_step(h - (halves - AHEAD))
    for c in range(halves, chunks):
        for d in range(1, n_re):
            x_copy(c, d).start()
    ph_copy = pltpu.make_async_copy(ph_hbm, ph, ph_sem)
    ph_copy.start()

    @pl.loop(AHEAD, chunks + (n_pb - 2) * (1 + SLACK))
    def _(t):
        @pl.when(t < chunks)
        def _():
            own_step(t)

        for d in range(1, n_pb - 1):
            c = t - d * (1 + SLACK)
            ok = (c >= 0) & (c < chunks)

            @pl.when(ok & (z - d >= 0) & (z < n_pb - 1))
            def _():
                z_copy(c, z - d, 1).wait_recv()
                z_copy(c, z - d, 1).start()

            @pl.when(ok & (z + d < n_pb) & (z > 0))
            def _():
                z_copy(c, z + d, 0).wait_recv()
                z_copy(c, z + d, 0).start()

    ph_copy.wait()
    q_tile = min(256, q_loc)

    @pl.loop(0, k_own)
    def _(k):
        for h in range(halves):
            for s in range(n_pb):
                @pl.when(((s < z) & (z == n_pb - 1)) | ((s > z) & (z == 0)))
                def _():
                    z_copy(k * halves + h, s, 0).wait_recv()

            spans = [slice(s * p_loc + h * p_half, s * p_loc + (h + 1) * p_half) for s in range(n_pb)]

            @pl.loop(0, q_loc // q_tile)
            def _(i):
                at = pl.ds(pl.multiple_of(i * q_tile, q_tile), q_tile)
                data = jnp.concatenate([gath[k, w, :] for w in spans], axis=0)
                cos_q = jnp.concatenate([ph[0, at, w] for w in spans], axis=1)
                sin_q = jnp.concatenate([ph[1, at, w] for w in spans], axis=1)
                by_cos = jnp.dot(cos_q, data, preferred_element_type=F32)
                by_sin = jnp.dot(sin_q, data, preferred_element_type=F32)
                real = by_cos[:, :b] - by_sin[:, b:]
                imag = by_cos[:, b:] + by_sin[:, :b]
                out[k, 0, at, :] = real if h == 0 else out[k, 0, at, :] + real
                out[k, 1, at, :] = imag if h == 0 else out[k, 1, at, :] + imag

    @pl.loop(0, chunks)
    def _(c):
        for d in range(1, n_re):
            @pl.when(c < halves)
            def _():
                x_first_copy(c, d).wait_send()

            @pl.when(c >= halves)
            def _():
                x_copy(c, d).wait_send()
        for s in range(n_pb):
            @pl.when((s >= z) & (z > 0))
            def _():
                z_copy(c, s, 0).wait_send()

            @pl.when((s <= z) & (z < n_pb - 1))
            def _():
                z_copy(c, s, 1).wait_send()


def body(n_re, n_pb, g_wann, phonon_phase, electron_phase):
    _, p_loc, e_loc, b = g_wann.shape
    _, q_loc, p_all = phonon_phase.shape
    k_all = electron_phase.shape[1]
    k_own = k_all // n_re
    halves = 2
    chunks = k_own * halves
    g = g_wann.reshape(2, p_loc * e_loc, b)
    far = pl.BlockSpec(memory_space=pltpu.HBM)
    near = pl.BlockSpec(memory_space=pltpu.VMEM)
    return pl.pallas_call(
        functools.partial(kernel, n_re, n_pb, halves),
        out_shape=jax.ShapeDtypeStruct((k_own, 2, q_loc, b), F32),
        in_specs=[far, far, far],
        out_specs=near,
        scratch_shapes=[
            pltpu.VMEM(g.shape, BF16),
            pltpu.VMEM(phonon_phase.shape, BF16),
            pltpu.VMEM(electron_phase.shape, BF16),
            pltpu.VMEM((2 * k_all * GROUP, 2 * GROUP * e_loc), BF16),
            pltpu.VMEM((k_all, p_loc, 2 * b), F32),
            pltpu.VMEM((n_re, p_loc, 2 * b), BF16),
            pltpu.VMEM((n_re - 1, p_loc, 2 * b), BF16),
            pltpu.VMEM((n_re - 1, k_own, p_loc, 2 * b), F32),
            pltpu.VMEM((k_own, p_all, 2 * b), BF16),
            pltpu.SemaphoreType.DMA((halves,)),
            pltpu.SemaphoreType.DMA,
            pltpu.SemaphoreType.DMA,
            pltpu.SemaphoreType.DMA((n_re - 1, chunks)),
            pltpu.SemaphoreType.DMA((n_re - 1, chunks)),
            pltpu.SemaphoreType.DMA((2, chunks, n_pb)),
            pltpu.SemaphoreType.DMA((chunks, n_pb)),
        ],
        compiler_params=pltpu.CompilerParams(
            collective_id=0, has_side_effects=True, vmem_limit_bytes=24 * 1024 * 1024
        ),
    )(*(pltpu.with_memory_space_constraint(a, pltpu.HBM) for a in (g, phonon_phase, electron_phase)))


def fold_kernel(
    n_re, n_pb, n_grp, n_ka, halves, early, ahead, pieces,
    g_hbm, ph_hbm, el_hbm, out,
    g, ph, el_ref, el_block, part, xs, xr, gath, far_ph, s_out, s_in,
    g_sem, ph_sem, el_sem, x_send, x_got, z_send, z_got, s_send, s_got,
    e1_send, e1_got, e2_send, e2_got, e3_send, e3_got,
):
    x = lax.axis_index("re")
    y = lax.axis_index("grp")
    z = lax.axis_index("pb")
    core = lax.axis_index("ka")
    chunks, p_loc, b = part.shape
    half_b = b // 2
    k_own = chunks // 2
    k_all = k_own * n_re
    p_half = p_loc // halves
    e_all = el_ref.shape[2]
    e_loc = g.shape[1] // p_loc
    q_loc = ph.shape[1]
    p_far = (n_pb - 1) * p_loc
    last = n_pb - 1

    lower = 2 * z < n_pb
    is_edge = (z == 0) | (z == last)
    is_inner = jnp.logical_not(is_edge)
    edge = jnp.where(lower, 0, last)
    far_edge = last - edge
    mate = last - z
    inward = jnp.where(lower, z + 1, z - 1)
    outward = jnp.where(lower, z - 1, z + 1)
    share = q_loc // (n_grp * n_ka)
    piece = share // pieces

    def g_copy(h):
        rows = pl.ds(h * p_half * e_loc, p_half * e_loc)
        return pltpu.make_async_copy(g_hbm.at[:, rows, :], g.at[:, rows, :], g_sem.at[h])

    barrier = pltpu.get_barrier_semaphore()
    for axis, at, n in (("re", x, n_re), ("grp", y, n_grp), ("ka", core, n_ka)):
        for d in range(1, n):
            pl.semaphore_signal(barrier, inc=1, device_id={axis: lax.rem(at + d, n)}, device_id_type=MESH)
    pl.semaphore_signal(barrier, inc=1, device_id={"pb": inward}, device_id_type=MESH)

    @pl.when(is_inner)
    def _():
        pl.semaphore_signal(barrier, inc=1, device_id={"pb": outward}, device_id_type=MESH)

    el_copy = pltpu.make_async_copy(el_hbm, el_ref, el_sem)
    el_copy.start()
    for h in range(halves):
        g_copy(h).start()

    rows, cols = k_all * GROUP, GROUP * e_loc
    place = iota((rows, k_all), 0) // GROUP
    owner = lax.rem(x + place // k_own, n_re)
    spread_k = (owner * k_own + place % k_own == iota((rows, k_all), 1)).astype(BF16)
    spread_e = (iota((e_all, cols), 0) == x * e_loc + iota((e_all, cols), 1) % e_loc).astype(BF16)
    same_p = iota((rows, cols), 0) % GROUP == iota((rows, cols), 1) // e_loc

    def spread(table):
        t = jnp.dot(spread_k, table, preferred_element_type=F32).astype(BF16)
        t = jnp.dot(t, spread_e, preferred_element_type=F32)
        return jnp.where(same_p, t, 0.0)

    el_copy.wait()
    cos_e = spread(el_ref[0])
    sin_e = spread(el_ref[1])
    el_block[0:rows, 0:cols] = cos_e.astype(BF16)
    el_block[0:rows, cols:] = (-sin_e).astype(BF16)
    el_block[rows:, 0:cols] = sin_e.astype(BF16)
    el_block[rows:, cols:] = cos_e.astype(BF16)

    def x_copy(c, h, d):
        there = pl.ds(pl.multiple_of(h * p_half, p_half), p_half)
        return pltpu.make_async_remote_copy(
            src_ref=xs.at[d - 1, c, there, :],
            dst_ref=xr.at[d - 1, c, there, :],
            send_sem=x_send.at[d - 1, c, h],
            recv_sem=x_got.at[d - 1, c, h],
            device_id={"re": lax.rem(x + d, n_re)},
            device_id_type=MESH,
        )

    def z_copy(c, source, way):
        there = pl.ds(pl.multiple_of(source * p_loc, p_loc), p_loc)
        block = gath.at[c, there, :]
        return pltpu.make_async_remote_copy(
            src_ref=block,
            dst_ref=block,
            send_sem=z_send.at[way, c, source],
            recv_sem=z_got.at[c, source],
            device_id={"pb": outward if way else inward},
            device_id_type=MESH,
        )

    def s_copy(c, i, to):
        at = pl.ds(pl.multiple_of(i * q_tile, q_tile), q_tile)
        return pltpu.make_async_remote_copy(
            src_ref=s_out.at[c - early, at, :],
            dst_ref=s_in.at[c - early, at, :],
            send_sem=s_send.at[c - early, i],
            recv_sem=s_got.at[c - early, i],
            device_id={"pb": to},
            device_id_type=MESH,
        )

    def span(of_y, of_core, i):
        first = (of_y * n_ka + of_core) * share + i * piece
        return pl.ds(pl.multiple_of(first, piece), piece)

    def e1_copy(i):
        at = span(y, core, i)
        wide = pl.ds(pl.multiple_of(jnp.where(lower, p_loc, 0), p_loc), p_far)
        return pltpu.make_async_remote_copy(
            src_ref=ph_hbm.at[:, at, wide],
            dst_ref=far_ph.at[:, at, :],
            send_sem=e1_send.at[i],
            recv_sem=e1_got.at[i],
            device_id={"pb": inward},
            device_id_type=MESH,
        )

    def e2_copy(d, i):
        block = far_ph.at[:, span(y, core, i), :]
        return pltpu.make_async_remote_copy(
            src_ref=block,
            dst_ref=block,
            send_sem=e2_send.at[d - 1, i],
            recv_sem=e2_got.at[d - 1, i],
            device_id={"grp": lax.rem(y + d, n_grp)},
            device_id_type=MESH,
        )

    def e3_copy(d, j, i):
        block = far_ph.at[:, span(lax.rem(y + n_grp - j, n_grp), core, i), :]
        return pltpu.make_async_remote_copy(
            src_ref=block,
            dst_ref=block,
            send_sem=e3_send.at[d - 1, j, i],
            recv_sem=e3_got.at[d - 1, j, i],
            device_id={"ka": lax.rem(core + d, n_ka)},
            device_id_type=MESH,
        )

    n_meet = n_re + n_grp + n_ka - 3 + jnp.where(is_edge, 1, 2)
    pl.semaphore_wait(barrier, n_meet)

    @pl.when(is_edge)
    def _():
        for i in range(pieces):
            e1_copy(i).start()

    left16 = iota((PAIR * GROUP, b), 1) < half_b
    for h in range(halves):
        g_copy(h).wait()

        @pl.loop(h * (p_half // GROUP // PAIR), (h + 1) * (p_half // GROUP // PAIR), unroll=UNROLL)
        def _(j):
            sides = []
            for side in range(PAIR):
                at = pl.ds(pl.multiple_of((j * PAIR + side) * cols, cols), cols)
                sides.append(jnp.concatenate([g[0, at, :], g[1, at, :]], axis=0))
            both = jnp.concatenate(sides, axis=1)
            res = jnp.dot(el_block[...], both, preferred_element_type=F32)
            p_at = pl.ds(pl.multiple_of(j * PAIR * GROUP, PAIR * GROUP), PAIR * GROUP)

            def piece_of(first):
                return jnp.concatenate(
                    [res[first:first + GROUP, s * b:(s + 1) * b] for s in range(PAIR)], axis=0
                )

            for d in range(n_re):
                for k in range(k_own):
                    real = piece_of((d * k_own + k) * GROUP)
                    imag = piece_of((k_all + d * k_own + k) * GROUP)
                    one = jnp.where(left16, real, pltpu.roll(imag, half_b, 1))
                    two = jnp.where(left16, pltpu.roll(real, half_b, 1), imag)
                    if d == 0:
                        part[2 * k, p_at, :] = one
                        part[2 * k + 1, p_at, :] = two
                    else:
                        xs[d - 1, 2 * k, p_at, :] = one.astype(BF16)
                        xs[d - 1, 2 * k + 1, p_at, :] = two.astype(BF16)

        if h < halves - 1:
            for d in range(1, n_re):
                x_copy(0, h, d).start()
    for d in range(1, n_re):
        x_copy(0, halves - 1, d).start()
    for c in range(1, chunks):
        for h in range(halves):
            for d in range(1, n_re):
                x_copy(c, h, d).start()
    ph_copy = pltpu.make_async_copy(ph_hbm, ph, ph_sem)
    ph_copy.start()

    mine = pl.ds(pl.multiple_of(z * p_loc, p_loc), p_loc)

    def own(c):
        total = part[c]
        for d in range(1, n_re):
            for h in range(halves):
                x_copy(c, h, d).wait_recv()
            total = total + xr[d - 1, c].astype(F32)
        gath[c, mine, :] = total.astype(BF16)
        z_copy(c, z, 0).start()

        @pl.when(is_inner & (c < early))
        def _():
            z_copy(c, z, 1).start()

    def relay_mate(c):
        @pl.when(is_inner)
        def _():
            z_copy(c, mate, 1).wait_recv()
            z_copy(c, mate, 1).start()

    def pass_piece(i):
        @pl.when(is_inner)
        def _():
            e1_copy(i).wait_recv()
            for d in range(1, n_grp):
                e2_copy(d, i).start()
            for d in range(1, n_ka):
                e3_copy(d, 0, i).start()

    for t in range(ahead):
        own(t)
        if 0 < t <= early:
            relay_mate(t - 1)
        if t < pieces:
            pass_piece(t)
    for c in range(ahead - 1, early):
        relay_mate(c)
    for i in range(ahead, pieces):
        pass_piece(i)

    @pl.when(is_edge)
    def _():
        @pl.loop(ahead, chunks)
        def _(c):
            own(c)

    ph_copy.wait()
    q_tile = min(256, q_loc)
    tiles = q_loc // q_tile
    left = iota((q_tile, b), 1) < half_b

    def rotate(by_cos, by_sin):
        turned = pltpu.roll(by_sin, half_b, 1)
        return by_cos + jnp.where(left, -turned, turned)

    def fold(c):
        data = gath[c, pl.ds(pl.multiple_of(jnp.where(lower, p_loc, 0), p_loc), p_far), :]

        @pl.loop(0, tiles)
        def _(i):
            at = pl.ds(pl.multiple_of(i * q_tile, q_tile), q_tile)
            by_cos = jnp.dot(far_ph[0, at, :], data, preferred_element_type=F32)
            by_sin = jnp.dot(far_ph[1, at, :], data, preferred_element_type=F32)
            s_out[c - early, at, :] = rotate(by_cos, by_sin).astype(BF16)
            s_copy(c, i, outward).start()

    def couple(c, cols_at, rows_at):
        k, s = c // 2, c % 2
        data = gath[c, rows_at, :]

        @pl.loop(0, tiles)
        def _(i):
            at = pl.ds(pl.multiple_of(i * q_tile, q_tile), q_tile)
            by_cos = jnp.dot(ph[0, at, cols_at], data, preferred_element_type=F32)
            by_sin = jnp.dot(ph[1, at, cols_at], data, preferred_element_type=F32)
            out[k, s, at, :] = rotate(by_cos, by_sin)

    def unmix(k):
        @pl.loop(0, tiles)
        def _(i):
            at = pl.ds(pl.multiple_of(i * q_tile, q_tile), q_tile)
            one = out[k, 0, at, :]
            two = out[k, 1, at, :]
            out[k, 0, at, :] = jnp.where(left, one, pltpu.roll(two, half_b, 1))
            out[k, 1, at, :] = jnp.where(left, pltpu.roll(one, half_b, 1), two)

    @pl.loop(0, chunks + LAG)
    def _(t):
        @pl.when(is_inner & (t < chunks))
        def _():
            @pl.when(t >= ahead)
            def _():
                own(t)

            z_copy(t, edge, 0).wait_recv()
            z_copy(t, edge, 0).start()

        for i in range(pieces):
            @pl.when(is_inner & (t == max(0, i - 1)))
            def _():
                for j in range(1, n_grp):
                    e2_copy(j, i).wait_recv()
                    for d in range(1, n_ka):
                        e3_copy(d, j, i).start()

        c = t - LAG

        @pl.when(is_inner & (c >= 0) & (c < early))
        def _():
            z_copy(c, far_edge, 1).wait_recv()
            z_copy(c, far_edge, 1).start()

        @pl.when(is_inner & (c == early))
        def _():
            for i in range(pieces):
                for d in range(1, n_ka):
                    for j in range(n_grp):
                        e3_copy(d, j, i).wait_recv()

        @pl.when(is_inner & (c >= early))
        def _():
            z_copy(c, mate, 1).wait_recv()
            z_copy(c, far_edge, 1).wait_recv()
            fold(c)

        @pl.when(is_edge & (c >= 0) & (c < early))
        def _():
            z_copy(c, inward, 0).wait_recv()
            z_copy(c, mate, 0).wait_recv()
            z_copy(c, jnp.where(lower, 2, last - 2), 0).wait_recv()

        @pl.when((c >= 0) & (is_inner | (c < early)))
        def _():
            couple(c, slice(None), slice(None))

            @pl.when(c % 2 == 1)
            def _():
                unmix(c // 2)

        @pl.when(is_edge & (c >= early))
        def _():
            couple(c, pl.ds(pl.multiple_of(z * p_loc, p_loc), p_loc), mine)

    @pl.when(is_edge)
    def _():
        @pl.loop(early, chunks)
        def _(c):
            k, s = c // 2, c % 2

            @pl.loop(0, tiles)
            def _(i):
                s_copy(c, i, inward).wait_recv()
                at = pl.ds(pl.multiple_of(i * q_tile, q_tile), q_tile)
                out[k, s, at, :] = out[k, s, at, :] + s_in[c - early, at, :].astype(F32)

            @pl.when(c % 2 == 1)
            def _():
                unmix(k)

        for i in range(pieces):
            e1_copy(i).wait_send()

    @pl.when(is_inner)
    def _():
        for i in range(pieces):
            for d in range(1, n_grp):
                e2_copy(d, i).wait_send()
            for d in range(1, n_ka):
                for j in range(n_grp):
                    e3_copy(d, j, i).wait_send()

        @pl.loop(0, chunks)
        def _(c):
            z_copy(c, edge, 0).wait_send()

            @pl.when(c < early)
            def _():
                z_copy(c, z, 1).wait_send()
                z_copy(c, mate, 1).wait_send()
                z_copy(c, far_edge, 1).wait_send()

            @pl.when(c >= early)
            def _():
                for i in range(tiles):
                    s_copy(c, i, outward).wait_send()

    @pl.loop(0, chunks)
    def _(c):
        for d in range(1, n_re):
            for h in range(halves):
                x_copy(c, h, d).wait_send()
        z_copy(c, z, 0).wait_send()


def fold_body(n_re, n_pb, n_grp, n_ka, g_wann, phonon_phase, electron_phase):
    _, p_loc, e_loc, b = g_wann.shape
    _, q_loc, p_all = phonon_phase.shape
    k_all = electron_phase.shape[1]
    k_own = k_all // n_re
    halves = 2
    chunks = 2 * k_own
    early = min(EARLY, chunks - 1)
    ahead = min(OWN_AHEAD, chunks)
    pieces = PIECES
    tiles = q_loc // min(256, q_loc)
    g = g_wann.reshape(2, p_loc * e_loc, b)
    far = pl.BlockSpec(memory_space=pltpu.HBM)
    near = pl.BlockSpec(memory_space=pltpu.VMEM)
    dma = pltpu.SemaphoreType.DMA
    return pl.pallas_call(
        functools.partial(fold_kernel, n_re, n_pb, n_grp, n_ka, halves, early, ahead, pieces),
        out_shape=jax.ShapeDtypeStruct((k_own, 2, q_loc, b), F32),
        in_specs=[far, far, far],
        out_specs=near,
        scratch_shapes=[
            pltpu.VMEM(g.shape, BF16),
            pltpu.VMEM(phonon_phase.shape, BF16),
            pltpu.VMEM(electron_phase.shape, BF16),
            pltpu.VMEM((2 * k_all * GROUP, 2 * GROUP * e_loc), BF16),
            pltpu.VMEM((chunks, p_loc, b), F32),
            pltpu.VMEM((n_re - 1, chunks, p_loc, b), BF16),
            pltpu.VMEM((n_re - 1, chunks, p_loc, b), BF16),
            pltpu.VMEM((chunks, p_all, b), BF16),
            pltpu.VMEM((2, q_loc, (n_pb - 1) * p_loc), BF16),
            pltpu.VMEM((chunks - early, q_loc, b), BF16),
            pltpu.VMEM((chunks - early, q_loc, b), BF16),
            dma((halves,)),
            dma,
            dma,
            dma((n_re - 1, chunks, halves)),
            dma((n_re - 1, chunks, halves)),
            dma((2, chunks, n_pb)),
            dma((chunks, n_pb)),
            dma((chunks - early, tiles)),
            dma((chunks - early, tiles)),
            dma((pieces,)),
            dma((pieces,)),
            dma((n_grp - 1, pieces)),
            dma((n_grp - 1, pieces)),
            dma((n_ka - 1, n_grp, pieces)),
            dma((n_ka - 1, n_grp, pieces)),
        ],
        compiler_params=pltpu.CompilerParams(
            collective_id=0, has_side_effects=True, vmem_limit_bytes=32 * 1024 * 1024
        ),
    )(*(pltpu.with_memory_space_constraint(a, pltpu.HBM) for a in (g, phonon_phase, electron_phase)))


def can_fold(sizes, g_wann, phonon_phase, electron_phase):
    _, p_loc, _, b = g_wann.shape
    _, q_loc, _ = phonon_phase.shape
    n_re, n_pb, n_grp, n_ka = sizes
    two_inner = n_pb - 2 == 2 and (n_pb - 1) * p_loc > q_loc
    many = min(n_re, n_grp, n_ka) > 1 and electron_phase.shape[1] // n_re >= 3
    return two_inner and many and p_loc % b == 0 and q_loc % (16 * PIECES * n_grp * n_ka) == 0


def local(sizes, *arrays):
    if can_fold(sizes, *arrays):
        return fold_body(*sizes, *arrays)
    return body(*sizes[:2], *arrays)


def solution(mesh):
    placed = (P(None, "pb", ("grp", "re"), "ka"), P(None, "pb", None), P())
    sizes = tuple(mesh.shape[axis] for axis in ("re", "pb", "grp", "ka"))
    return jax.shard_map(
        functools.partial(local, sizes),
        mesh=mesh,
        in_specs=placed,
        out_specs=P(("grp", "re"), None, "pb", "ka"),
        check_vma=False,
    )
```

```python
import functools
import jax
import jax.numpy as jnp
from jax import lax
from jax.experimental import pallas as pl
from jax.experimental.pallas import tpu as pltpu
from jax.sharding import PartitionSpec as P

MESH = pl.DeviceIdType.MESH
GROUP = 8
PAIR = 2
UNROLL = 8
AHEAD = 1
SLACK = 0
EARLY = 4
OWN_AHEAD = 5
PIECES = 4
PASS_AT = (0, 1, 2, 3)
LAG = 2
SPREAD_AT = (0, 1, 2, 3)
BF16 = jnp.bfloat16
F32 = jnp.float32


def iota(shape, dim):
    return lax.broadcasted_iota(jnp.int32, shape, dim)


def kernel(
    n_re, n_pb, halves,
    g_hbm, ph_hbm, el_hbm, out,
    g, ph, el_ref, el_block, part, x_first, x_first_recv, x_recv, gath,
    g_sem, ph_sem, el_sem, x_send, x_got, z_send, z_got,
):
    x = lax.axis_index("re")
    z = lax.axis_index("pb")
    k_all, p_loc, width = part.shape
    b = width // 2
    k_own = k_all // n_re
    p_half = p_loc // halves
    e_all = el_ref.shape[2]
    e_loc = g.shape[1] // p_loc
    chunks = k_own * halves
    q_loc = ph.shape[1]

    def g_copy(h):
        rows = pl.ds(h * p_half * e_loc, p_half * e_loc)
        return pltpu.make_async_copy(g_hbm.at[:, rows, :], g.at[:, rows, :], g_sem.at[h])

    barrier = pltpu.get_barrier_semaphore()
    for d in range(1, n_re):
        pl.semaphore_signal(barrier, inc=1, device_id={"re": lax.rem(x + d, n_re)}, device_id_type=MESH)

    @pl.when(z > 0)
    def _():
        pl.semaphore_signal(barrier, inc=1, device_id={"pb": z - 1}, device_id_type=MESH)

    @pl.when(z < n_pb - 1)
    def _():
        pl.semaphore_signal(barrier, inc=1, device_id={"pb": z + 1}, device_id_type=MESH)

    el_copy = pltpu.make_async_copy(el_hbm, el_ref, el_sem)
    el_copy.start()
    for h in range(halves):
        g_copy(h).start()

    rows, cols = k_all * GROUP, GROUP * e_loc
    spread_k = (iota((rows, k_all), 0) // GROUP == iota((rows, k_all), 1)).astype(BF16)
    spread_e = (iota((e_all, cols), 0) == x * e_loc + iota((e_all, cols), 1) % e_loc).astype(BF16)
    same_p = iota((rows, cols), 0) % GROUP == iota((rows, cols), 1) // e_loc

    def spread(table):
        t = jnp.dot(spread_k, table, preferred_element_type=F32).astype(BF16)
        t = jnp.dot(t, spread_e, preferred_element_type=F32)
        return jnp.where(same_p, t, 0.0)

    el_copy.wait()
    cos_e = spread(el_ref[0])
    sin_e = spread(el_ref[1])
    el_block[0:rows, 0:cols] = cos_e.astype(BF16)
    el_block[0:rows, cols:] = (-sin_e).astype(BF16)
    el_block[rows:, 0:cols] = sin_e.astype(BF16)
    el_block[rows:, cols:] = cos_e.astype(BF16)

    def x_first_copy(h, d):
        there = pl.ds(pl.multiple_of(h * p_half, p_half), p_half)
        to = lax.rem(x + d, n_re)
        return pltpu.make_async_remote_copy(
            src_ref=x_first.at[to, there, :],
            dst_ref=x_first_recv.at[d - 1, there, :],
            send_sem=x_send.at[d - 1, h],
            recv_sem=x_got.at[d - 1, h],
            device_id={"re": to},
            device_id_type=MESH,
        )

    def x_copy(c, d):
        k, h = c // halves, c % halves
        there = pl.ds(pl.multiple_of(h * p_half, p_half), p_half)
        to = lax.rem(x + d, n_re)
        return pltpu.make_async_remote_copy(
            src_ref=part.at[to * k_own + k, there, :],
            dst_ref=x_recv.at[d - 1, k, there, :],
            send_sem=x_send.at[d - 1, c],
            recv_sem=x_got.at[d - 1, c],
            device_id={"re": to},
            device_id_type=MESH,
        )

    def z_copy(c, source, way):
        k, h = c // halves, c % halves
        there = pl.ds(pl.multiple_of(source * p_loc + h * p_half, p_half), p_half)
        block = gath.at[k, there, :]
        return pltpu.make_async_remote_copy(
            src_ref=block,
            dst_ref=block,
            send_sem=z_send.at[way, c, source],
            recv_sem=z_got.at[c, source],
            device_id={"pb": z + 1 if way else z - 1},
            device_id_type=MESH,
        )

    def own_step(t):
        k, h = t // halves, t % halves
        there = pl.ds(pl.multiple_of(h * p_half, p_half), p_half)
        mine = pl.ds(pl.multiple_of(z * p_loc + h * p_half, p_half), p_half)

        @pl.when(t < halves)
        def _():
            total = part[x * k_own, there, :]
            for d in range(1, n_re):
                x_first_copy(t, d).wait_recv()
                total = total + x_first_recv[d - 1, there, :].astype(F32)
            gath[0, mine, :] = total.astype(BF16)

        @pl.when(t >= halves)
        def _():
            total = part[x * k_own + k, there, :]
            for d in range(1, n_re):
                x_copy(t, d).wait_recv()
                total = total + x_recv[d - 1, k, there, :]
            gath[k, mine, :] = total.astype(BF16)

        @pl.when(z > 0)
        def _():
            z_copy(t, z, 0).start()

        @pl.when(z < n_pb - 1)
        def _():
            z_copy(t, z, 1).start()

    for h in range(halves):
        g_copy(h).wait()

        @pl.loop(h * (p_half // GROUP // PAIR), (h + 1) * (p_half // GROUP // PAIR), unroll=UNROLL)
        def _(j):
            sides = []
            for side in range(PAIR):
                at = pl.ds(pl.multiple_of((j * PAIR + side) * cols, cols), cols)
                sides.append(jnp.concatenate([g[0, at, :], g[1, at, :]], axis=0))
            both = jnp.concatenate(sides, axis=1)
            res = jnp.dot(el_block[...], both, preferred_element_type=F32)
            for side in range(PAIR):
                p_at = pl.ds(pl.multiple_of((j * PAIR + side) * GROUP, GROUP), GROUP)
                for c in range(2):
                    for k in range(k_all):
                        first = (c * k_all + k) * GROUP
                        part[k, p_at, c * b:(c + 1) * b] = res[first:first + GROUP, side * b:(side + 1) * b]

        if h == 0:
            n_meet = n_re - 1 + jnp.where(z > 0, 1, 0) + jnp.where(z < n_pb - 1, 1, 0)
            pl.semaphore_wait(barrier, n_meet)
        there = pl.ds(h * p_half, p_half)
        for r in range(n_re):
            x_first[r, there, :] = part[r * k_own, there, :].astype(BF16)
        for d in range(1, n_re):
            x_first_copy(h, d).start()
        if h >= halves - AHEAD:
            own_step(h - (halves - AHEAD))
    for c in range(halves, chunks):
        for d in range(1, n_re):
            x_copy(c, d).start()
    ph_copy = pltpu.make_async_copy(ph_hbm, ph, ph_sem)
    ph_copy.start()

    @pl.loop(AHEAD, chunks + (n_pb - 2) * (1 + SLACK))
    def _(t):
        @pl.when(t < chunks)
        def _():
            own_step(t)

        for d in range(1, n_pb - 1):
            c = t - d * (1 + SLACK)
            ok = (c >= 0) & (c < chunks)

            @pl.when(ok & (z - d >= 0) & (z < n_pb - 1))
            def _():
                z_copy(c, z - d, 1).wait_recv()
                z_copy(c, z - d, 1).start()

            @pl.when(ok & (z + d < n_pb) & (z > 0))
            def _():
                z_copy(c, z + d, 0).wait_recv()
                z_copy(c, z + d, 0).start()

    ph_copy.wait()
    q_tile = min(256, q_loc)

    @pl.loop(0, k_own)
    def _(k):
        for h in range(halves):
            for s in range(n_pb):
                @pl.when(((s < z) & (z == n_pb - 1)) | ((s > z) & (z == 0)))
                def _():
                    z_copy(k * halves + h, s, 0).wait_recv()

            spans = [slice(s * p_loc + h * p_half, s * p_loc + (h + 1) * p_half) for s in range(n_pb)]

            @pl.loop(0, q_loc // q_tile)
            def _(i):
                at = pl.ds(pl.multiple_of(i * q_tile, q_tile), q_tile)
                data = jnp.concatenate([gath[k, w, :] for w in spans], axis=0)
                cos_q = jnp.concatenate([ph[0, at, w] for w in spans], axis=1)
                sin_q = jnp.concatenate([ph[1, at, w] for w in spans], axis=1)
                by_cos = jnp.dot(cos_q, data, preferred_element_type=F32)
                by_sin = jnp.dot(sin_q, data, preferred_element_type=F32)
                real = by_cos[:, :b] - by_sin[:, b:]
                imag = by_cos[:, b:] + by_sin[:, :b]
                out[k, 0, at, :] = real if h == 0 else out[k, 0, at, :] + real
                out[k, 1, at, :] = imag if h == 0 else out[k, 1, at, :] + imag

    @pl.loop(0, chunks)
    def _(c):
        for d in range(1, n_re):
            @pl.when(c < halves)
            def _():
                x_first_copy(c, d).wait_send()

            @pl.when(c >= halves)
            def _():
                x_copy(c, d).wait_send()
        for s in range(n_pb):
            @pl.when((s >= z) & (z > 0))
            def _():
                z_copy(c, s, 0).wait_send()

            @pl.when((s <= z) & (z < n_pb - 1))
            def _():
                z_copy(c, s, 1).wait_send()


def body(n_re, n_pb, g_wann, phonon_phase, electron_phase):
    _, p_loc, e_loc, b = g_wann.shape
    _, q_loc, p_all = phonon_phase.shape
    k_all = electron_phase.shape[1]
    k_own = k_all // n_re
    halves = 2
    chunks = k_own * halves
    g = g_wann.reshape(2, p_loc * e_loc, b)
    far = pl.BlockSpec(memory_space=pltpu.HBM)
    near = pl.BlockSpec(memory_space=pltpu.VMEM)
    return pl.pallas_call(
        functools.partial(kernel, n_re, n_pb, halves),
        out_shape=jax.ShapeDtypeStruct((k_own, 2, q_loc, b), F32),
        in_specs=[far, far, far],
        out_specs=near,
        scratch_shapes=[
            pltpu.VMEM(g.shape, BF16),
            pltpu.VMEM(phonon_phase.shape, BF16),
            pltpu.VMEM(electron_phase.shape, BF16),
            pltpu.VMEM((2 * k_all * GROUP, 2 * GROUP * e_loc), BF16),
            pltpu.VMEM((k_all, p_loc, 2 * b), F32),
            pltpu.VMEM((n_re, p_loc, 2 * b), BF16),
            pltpu.VMEM((n_re - 1, p_loc, 2 * b), BF16),
            pltpu.VMEM((n_re - 1, k_own, p_loc, 2 * b), F32),
            pltpu.VMEM((k_own, p_all, 2 * b), BF16),
            pltpu.SemaphoreType.DMA((halves,)),
            pltpu.SemaphoreType.DMA,
            pltpu.SemaphoreType.DMA,
            pltpu.SemaphoreType.DMA((n_re - 1, chunks)),
            pltpu.SemaphoreType.DMA((n_re - 1, chunks)),
            pltpu.SemaphoreType.DMA((2, chunks, n_pb)),
            pltpu.SemaphoreType.DMA((chunks, n_pb)),
        ],
        compiler_params=pltpu.CompilerParams(
            collective_id=0, has_side_effects=True, vmem_limit_bytes=24 * 1024 * 1024
        ),
    )(*(pltpu.with_memory_space_constraint(a, pltpu.HBM) for a in (g, phonon_phase, electron_phase)))


def fold_kernel(
    n_re, n_pb, n_grp, n_ka, halves, early, ahead, pieces,
    g_hbm, ph_hbm, el_hbm, out,
    g, ph, el_ref, el_block, part, xs, xr, gath, far_ph, s_out, s_in,
    g_sem, ph_sem, el_sem, x_send, x_got, z_send, z_got, s_send, s_got,
    e1_send, e1_got, e2_send, e2_got, e3_send, e3_got,
):
    x = lax.axis_index("re")
    y = lax.axis_index("grp")
    z = lax.axis_index("pb")
    core = lax.axis_index("ka")
    chunks, p_loc, b = part.shape
    half_b = b // 2
    k_own = chunks // 2
    k_all = k_own * n_re
    p_half = p_loc // halves
    e_all = el_ref.shape[2]
    e_loc = g.shape[1] // p_loc
    q_loc = ph.shape[1]
    p_far = (n_pb - 1) * p_loc
    last = n_pb - 1

    lower = 2 * z < n_pb
    is_edge = (z == 0) | (z == last)
    is_inner = jnp.logical_not(is_edge)
    edge = jnp.where(lower, 0, last)
    far_edge = last - edge
    mate = last - z
    inward = jnp.where(lower, z + 1, z - 1)
    outward = jnp.where(lower, z - 1, z + 1)
    share = q_loc // (n_grp * n_ka)
    piece = share // pieces

    def g_copy(h):
        rows = pl.ds(h * p_half * e_loc, p_half * e_loc)
        return pltpu.make_async_copy(g_hbm.at[:, rows, :], g.at[:, rows, :], g_sem.at[h])

    barrier = pltpu.get_barrier_semaphore()
    for axis, at, n in (("re", x, n_re), ("grp", y, n_grp), ("ka", core, n_ka)):
        for d in range(1, n):
            pl.semaphore_signal(barrier, inc=1, device_id={axis: lax.rem(at + d, n)}, device_id_type=MESH)
    pl.semaphore_signal(barrier, inc=1, device_id={"pb": inward}, device_id_type=MESH)

    @pl.when(is_inner)
    def _():
        pl.semaphore_signal(barrier, inc=1, device_id={"pb": outward}, device_id_type=MESH)

    el_copy = pltpu.make_async_copy(el_hbm, el_ref, el_sem)
    el_copy.start()
    for h in range(halves):
        g_copy(h).start()

    rows, cols = k_all * GROUP, GROUP * e_loc
    place = iota((rows, k_all), 0) // GROUP
    owner = lax.rem(x + place // k_own, n_re)
    spread_k = (owner * k_own + place % k_own == iota((rows, k_all), 1)).astype(BF16)
    spread_e = (iota((e_all, cols), 0) == x * e_loc + iota((e_all, cols), 1) % e_loc).astype(BF16)
    same_p = iota((rows, cols), 0) % GROUP == iota((rows, cols), 1) // e_loc

    def spread(table):
        t = jnp.dot(spread_k, table, preferred_element_type=F32).astype(BF16)
        t = jnp.dot(t, spread_e, preferred_element_type=F32)
        return jnp.where(same_p, t, 0.0)

    el_copy.wait()
    cos_e = spread(el_ref[0])
    sin_e = spread(el_ref[1])
    el_block[0:rows, 0:cols] = cos_e.astype(BF16)
    el_block[0:rows, cols:] = (-sin_e).astype(BF16)
    el_block[rows:, 0:cols] = sin_e.astype(BF16)
    el_block[rows:, cols:] = cos_e.astype(BF16)

    def x_copy(c, h, d):
        there = pl.ds(pl.multiple_of(h * p_half, p_half), p_half)
        return pltpu.make_async_remote_copy(
            src_ref=xs.at[d - 1, c, there, :],
            dst_ref=xr.at[d - 1, c, there, :],
            send_sem=x_send.at[d - 1, c, h],
            recv_sem=x_got.at[d - 1, c, h],
            device_id={"re": lax.rem(x + d, n_re)},
            device_id_type=MESH,
        )

    def z_copy(c, h, source, way):
        there = pl.ds(pl.multiple_of(source * p_loc + h * p_half, p_half), p_half)
        block = gath.at[c, there, :]
        return pltpu.make_async_remote_copy(
            src_ref=block,
            dst_ref=block,
            send_sem=z_send.at[way, c, h, source],
            recv_sem=z_got.at[c, h, source],
            device_id={"pb": outward if way else inward},
            device_id_type=MESH,
        )

    def z_got_all(c, source):
        for h in range(halves):
            z_copy(c, h, source, 0).wait_recv()

    def z_sent_all(c, source, way):
        for h in range(halves):
            z_copy(c, h, source, way).wait_send()

    def z_relay(c, source, way):
        for h in range(halves):
            z_copy(c, h, source, way).wait_recv()
            z_copy(c, h, source, way).start()

    def s_copy(c, i, to):
        at = pl.ds(pl.multiple_of(i * q_tile, q_tile), q_tile)
        return pltpu.make_async_remote_copy(
            src_ref=s_out.at[c - early, at, :],
            dst_ref=s_in.at[c - early, at, :],
            send_sem=s_send.at[c - early, i],
            recv_sem=s_got.at[c - early, i],
            device_id={"pb": to},
            device_id_type=MESH,
        )

    def span(of_y, of_core, i):
        first = (of_y * n_ka + of_core) * share + i * piece
        return pl.ds(pl.multiple_of(first, piece), piece)

    def e1_copy(i):
        at = span(y, core, i)
        wide = pl.ds(pl.multiple_of(jnp.where(lower, p_loc, 0), p_loc), p_far)
        return pltpu.make_async_remote_copy(
            src_ref=ph_hbm.at[:, at, wide],
            dst_ref=far_ph.at[:, at, :],
            send_sem=e1_send.at[i],
            recv_sem=e1_got.at[i],
            device_id={"pb": inward},
            device_id_type=MESH,
        )

    def e2_copy(d, i):
        block = far_ph.at[:, span(y, core, i), :]
        return pltpu.make_async_remote_copy(
            src_ref=block,
            dst_ref=block,
            send_sem=e2_send.at[d - 1, i],
            recv_sem=e2_got.at[d - 1, i],
            device_id={"grp": lax.rem(y + d, n_grp)},
            device_id_type=MESH,
        )

    def e3_copy(d, j, i):
        block = far_ph.at[:, span(lax.rem(y + n_grp - j, n_grp), core, i), :]
        return pltpu.make_async_remote_copy(
            src_ref=block,
            dst_ref=block,
            send_sem=e3_send.at[d - 1, j, i],
            recv_sem=e3_got.at[d - 1, j, i],
            device_id={"ka": lax.rem(core + d, n_ka)},
            device_id_type=MESH,
        )

    n_meet = n_re + n_grp + n_ka - 3 + jnp.where(is_edge, 1, 2)
    pl.semaphore_wait(barrier, n_meet)

    @pl.when(is_edge)
    def _():
        for i in range(pieces):
            e1_copy(i).start()

    left16 = iota((PAIR * GROUP, b), 1) < half_b
    for h in range(halves):
        g_copy(h).wait()

        @pl.loop(h * (p_half // GROUP // PAIR), (h + 1) * (p_half // GROUP // PAIR), unroll=UNROLL)
        def _(j):
            sides = []
            for side in range(PAIR):
                at = pl.ds(pl.multiple_of((j * PAIR + side) * cols, cols), cols)
                sides.append(jnp.concatenate([g[0, at, :], g[1, at, :]], axis=0))
            both = jnp.concatenate(sides, axis=1)
            res = jnp.dot(el_block[...], both, preferred_element_type=F32)
            p_at = pl.ds(pl.multiple_of(j * PAIR * GROUP, PAIR * GROUP), PAIR * GROUP)

            def piece_of(first):
                return jnp.concatenate(
                    [res[first:first + GROUP, s * b:(s + 1) * b] for s in range(PAIR)], axis=0
                )

            for d in range(n_re):
                for k in range(k_own):
                    real = piece_of((d * k_own + k) * GROUP)
                    imag = piece_of((k_all + d * k_own + k) * GROUP)
                    one = jnp.where(left16, real, pltpu.roll(imag, half_b, 1))
                    two = jnp.where(left16, pltpu.roll(real, half_b, 1), imag)
                    if d == 0:
                        part[2 * k, p_at, :] = one
                        part[2 * k + 1, p_at, :] = two
                    else:
                        xs[d - 1, 2 * k, p_at, :] = one.astype(BF16)
                        xs[d - 1, 2 * k + 1, p_at, :] = two.astype(BF16)

        if h < halves - 1:
            for d in range(1, n_re):
                x_copy(0, h, d).start()
    for d in range(1, n_re):
        x_copy(0, halves - 1, d).start()
    for c in range(1, chunks):
        for h in range(halves):
            for d in range(1, n_re):
                x_copy(c, h, d).start()
    ph_copy = pltpu.make_async_copy(ph_hbm, ph, ph_sem)
    ph_copy.start()

    mine = pl.ds(pl.multiple_of(z * p_loc, p_loc), p_loc)

    def own(c):
        for h in range(halves):
            there = slice(h * p_half, (h + 1) * p_half)
            total = part[c, there, :]
            for d in range(1, n_re):
                x_copy(c, h, d).wait_recv()
                total = total + xr[d - 1, c, there, :].astype(F32)
            at = pl.ds(pl.multiple_of(z * p_loc + h * p_half, p_half), p_half)
            gath[c, at, :] = total.astype(BF16)
            z_copy(c, h, z, 0).start()

            @pl.when(is_inner & (c < early))
            def _():
                z_copy(c, h, z, 1).start()

    def relay_mate(c):
        @pl.when(is_inner)
        def _():
            z_relay(c, mate, 1)

    def pass_piece(i):
        @pl.when(is_inner)
        def _():
            e1_copy(i).wait_recv()
            for d in range(1, n_grp):
                e2_copy(d, i).start()
            for d in range(1, n_ka):
                e3_copy(d, 0, i).start()

    for t in range(ahead):
        own(t)
        if 0 < t <= early:
            relay_mate(t - 1)
        for i in range(pieces):
            if PASS_AT[i] == t:
                pass_piece(i)
    for c in range(ahead - 1, early):
        relay_mate(c)

    @pl.when(is_edge)
    def _():
        @pl.loop(ahead, chunks)
        def _(c):
            own(c)

    ph_copy.wait()
    q_tile = min(256, q_loc)
    tiles = q_loc // q_tile
    left = iota((q_tile, b), 1) < half_b

    def rotate(by_cos, by_sin):
        turned = pltpu.roll(by_sin, half_b, 1)
        return by_cos + jnp.where(left, -turned, turned)

    def fold(c):
        data = gath[c, pl.ds(pl.multiple_of(jnp.where(lower, p_loc, 0), p_loc), p_far), :]

        @pl.loop(0, tiles)
        def _(i):
            at = pl.ds(pl.multiple_of(i * q_tile, q_tile), q_tile)
            by_cos = jnp.dot(far_ph[0, at, :], data, preferred_element_type=F32)
            by_sin = jnp.dot(far_ph[1, at, :], data, preferred_element_type=F32)
            s_out[c - early, at, :] = rotate(by_cos, by_sin).astype(BF16)
            s_copy(c, i, outward).start()

    def couple(c, cols_at, rows_at):
        k, s = c // 2, c % 2
        data = gath[c, rows_at, :]

        @pl.loop(0, tiles)
        def _(i):
            at = pl.ds(pl.multiple_of(i * q_tile, q_tile), q_tile)
            by_cos = jnp.dot(ph[0, at, cols_at], data, preferred_element_type=F32)
            by_sin = jnp.dot(ph[1, at, cols_at], data, preferred_element_type=F32)
            out[k, s, at, :] = rotate(by_cos, by_sin)

    def unmix(k):
        @pl.loop(0, tiles)
        def _(i):
            at = pl.ds(pl.multiple_of(i * q_tile, q_tile), q_tile)
            one = out[k, 0, at, :]
            two = out[k, 1, at, :]
            out[k, 0, at, :] = jnp.where(left, one, pltpu.roll(two, half_b, 1))
            out[k, 1, at, :] = jnp.where(left, pltpu.roll(one, half_b, 1), two)

    @pl.loop(0, chunks + LAG)
    def _(t):
        @pl.when(is_inner & (t < chunks))
        def _():
            @pl.when(t >= ahead)
            def _():
                own(t)

            z_relay(t, edge, 0)

        for i in range(pieces):
            @pl.when(is_inner & (t == SPREAD_AT[i]))
            def _():
                for j in range(1, n_grp):
                    e2_copy(j, i).wait_recv()
                    for d in range(1, n_ka):
                        e3_copy(d, j, i).start()

        c = t - LAG

        @pl.when(is_inner & (c >= 0) & (c < early))
        def _():
            z_relay(c, far_edge, 1)

        @pl.when(is_inner & (c == early))
        def _():
            for i in range(pieces):
                for d in range(1, n_ka):
                    for j in range(n_grp):
                        e3_copy(d, j, i).wait_recv()

        @pl.when(is_inner & (c >= early))
        def _():
            z_got_all(c, mate)
            z_got_all(c, far_edge)
            fold(c)

        @pl.when(is_edge & (c >= 0) & (c < early))
        def _():
            z_got_all(c, inward)
            z_got_all(c, mate)
            z_got_all(c, jnp.where(lower, 2, last - 2))

        @pl.when((c >= 0) & (is_inner | (c < early)))
        def _():
            couple(c, slice(None), slice(None))

            @pl.when(c % 2 == 1)
            def _():
                unmix(c // 2)

        @pl.when(is_edge & (c >= early))
        def _():
            couple(c, pl.ds(pl.multiple_of(z * p_loc, p_loc), p_loc), mine)

    @pl.when(is_edge)
    def _():
        @pl.loop(early, chunks)
        def _(c):
            k, s = c // 2, c % 2

            @pl.loop(0, tiles)
            def _(i):
                s_copy(c, i, inward).wait_recv()
                at = pl.ds(pl.multiple_of(i * q_tile, q_tile), q_tile)
                out[k, s, at, :] = out[k, s, at, :] + s_in[c - early, at, :].astype(F32)

            @pl.when(c % 2 == 1)
            def _():
                unmix(k)

        for i in range(pieces):
            e1_copy(i).wait_send()

    @pl.when(is_inner)
    def _():
        for i in range(pieces):
            for d in range(1, n_grp):
                e2_copy(d, i).wait_send()
            for d in range(1, n_ka):
                for j in range(n_grp):
                    e3_copy(d, j, i).wait_send()

        @pl.loop(0, chunks)
        def _(c):
            z_sent_all(c, edge, 0)

            @pl.when(c < early)
            def _():
                z_sent_all(c, z, 1)
                z_sent_all(c, mate, 1)
                z_sent_all(c, far_edge, 1)

            @pl.when(c >= early)
            def _():
                for i in range(tiles):
                    s_copy(c, i, outward).wait_send()

    @pl.loop(0, chunks)
    def _(c):
        for d in range(1, n_re):
            for h in range(halves):
                x_copy(c, h, d).wait_send()
        z_sent_all(c, z, 0)


def fold_body(n_re, n_pb, n_grp, n_ka, g_wann, phonon_phase, electron_phase):
    _, p_loc, e_loc, b = g_wann.shape
    _, q_loc, p_all = phonon_phase.shape
    k_all = electron_phase.shape[1]
    k_own = k_all // n_re
    halves = 2
    chunks = 2 * k_own
    early = min(EARLY, chunks - 1)
    ahead = min(OWN_AHEAD, chunks)
    pieces = PIECES
    tiles = q_loc // min(256, q_loc)
    g = g_wann.reshape(2, p_loc * e_loc, b)
    far = pl.BlockSpec(memory_space=pltpu.HBM)
    near = pl.BlockSpec(memory_space=pltpu.VMEM)
    dma = pltpu.SemaphoreType.DMA
    return pl.pallas_call(
        functools.partial(fold_kernel, n_re, n_pb, n_grp, n_ka, halves, early, ahead, pieces),
        out_shape=jax.ShapeDtypeStruct((k_own, 2, q_loc, b), F32),
        in_specs=[far, far, far],
        out_specs=near,
        scratch_shapes=[
            pltpu.VMEM(g.shape, BF16),
            pltpu.VMEM(phonon_phase.shape, BF16),
            pltpu.VMEM(electron_phase.shape, BF16),
            pltpu.VMEM((2 * k_all * GROUP, 2 * GROUP * e_loc), BF16),
            pltpu.VMEM((chunks, p_loc, b), F32),
            pltpu.VMEM((n_re - 1, chunks, p_loc, b), BF16),
            pltpu.VMEM((n_re - 1, chunks, p_loc, b), BF16),
            pltpu.VMEM((chunks, p_all, b), BF16),
            pltpu.VMEM((2, q_loc, (n_pb - 1) * p_loc), BF16),
            pltpu.VMEM((chunks - early, q_loc, b), BF16),
            pltpu.VMEM((chunks - early, q_loc, b), BF16),
            dma((halves,)),
            dma,
            dma,
            dma((n_re - 1, chunks, halves)),
            dma((n_re - 1, chunks, halves)),
            dma((2, chunks, halves, n_pb)),
            dma((chunks, halves, n_pb)),
            dma((chunks - early, tiles)),
            dma((chunks - early, tiles)),
            dma((pieces,)),
            dma((pieces,)),
            dma((n_grp - 1, pieces)),
            dma((n_grp - 1, pieces)),
            dma((n_ka - 1, n_grp, pieces)),
            dma((n_ka - 1, n_grp, pieces)),
        ],
        compiler_params=pltpu.CompilerParams(
            collective_id=0, has_side_effects=True, vmem_limit_bytes=32 * 1024 * 1024
        ),
    )(*(pltpu.with_memory_space_constraint(a, pltpu.HBM) for a in (g, phonon_phase, electron_phase)))


def can_fold(sizes, g_wann, phonon_phase, electron_phase):
    _, p_loc, _, b = g_wann.shape
    _, q_loc, _ = phonon_phase.shape
    n_re, n_pb, n_grp, n_ka = sizes
    two_inner = n_pb - 2 == 2 and (n_pb - 1) * p_loc > q_loc
    many = min(n_re, n_grp, n_ka) > 1 and electron_phase.shape[1] // n_re >= 3
    return two_inner and many and p_loc % b == 0 and q_loc % (16 * PIECES * n_grp * n_ka) == 0


def local(sizes, *arrays):
    if can_fold(sizes, *arrays):
        return fold_body(*sizes, *arrays)
    return body(*sizes[:2], *arrays)


def solution(mesh):
    placed = (P(None, "pb", ("grp", "re"), "ka"), P(None, "pb", None), P())
    sizes = tuple(mesh.shape[axis] for axis in ("re", "pb", "grp", "ka"))
    return jax.shard_map(
        functools.partial(local, sizes),
        mesh=mesh,
        in_specs=placed,
        out_specs=P(("grp", "re"), None, "pb", "ka"),
        check_vma=False,
    )
```
